32 devices in a mesh: terms: 8 (over z, y), sect: 4 (over x, core).
Axes of the slice: x: 2, y: 2, z: 4, core: 2. Of those that a mesh axis runs over, the one named last changes fastest.
Arguments:
- wavefunction: float32 [2, 512, 16, 512], P(None, 'sect'), may hold values from -6 to 6
- left_blocks: float32 [8, 2, 512, 128], P('terms', None, 'sect'), may hold values from -0.125 to 0.125
- right_operators: float32 [8, 2, 512, 512], P('terms'), may hold values from -0.1875 to 0.1875
- site_operators: float32 [8, 2, 16, 16], P('terms'), may hold values from -1 to 1
- term_charge: int32 [8], replicated, may hold values from 0 to 1
- source_terms: int32 [8, 3], replicated, may hold values from 0 to 7, all different within a row
- coupling: float32 [2, 8, 3], replicated, may hold values from -0.01953125 to 0.01953125
- owner: int32 [8], replicated, may hold values from 0 to 7, each once
Outputs:
- sigma: float32 [2, 512, 16, 512], P(None, 'sect', None, 'terms')
- new_right: float32 [8, 2, 512, 128], P('terms', None, 'sect')
The draws below stay inside these ranges and needn't reach their ends.
Inputs may be any that keep to these rules, and one draw needn't show every extreme that they name: `source_terms`: each row names 3 different terms, and every term is named by some row. `owner`: each index along terms owns exactly one new term.
All inputs are finite; a program needn't handle non-finite values.
Results may differ from the reference program's by a relative error of at most 0.0003.
Values sent between devices are 32-bit elements; how exact they have to be, the bound alone decides.
A program may use at most 128 MiB of HBM per device.

```python
import jax
import jax.numpy as jnp
from jax import lax

BOND = 512
PHYS = 16
TOP = 3
K = 8
MB = 128


def plant(drawn, stream_key, low, high):
    longest = drawn.shape.index(max(drawn.shape))
    spots = []
    for shift in (0, 1):
        where = [jax.random.randint(jax.random.fold_in(stream_key, axis), (), 0, length) for axis, length in enumerate(drawn.shape)]
        where[longest] = (where[longest] + shift) % drawn.shape[longest]
        spots.append(tuple(where))
    return drawn.at[spots[0]].set(low).at[spots[1]].set(high)


def levels(rng, shape, split, least, largest):
    gain = 1.0
    for position, blocks in split:
        draws = jax.random.uniform(jax.random.fold_in(jax.random.fold_in(rng, 6), position), (blocks,), jnp.float32, least / len(split), largest / len(split))
        gain = gain * jnp.repeat(jnp.exp(draws), shape[position] // blocks).reshape((-1,) + (1,) * (len(shape) - 1 - position))
    return gain


def distinct(stream_key, rows, amount, top, lift):
    ranking = jax.random.permutation(jax.random.fold_in(stream_key, 1), amount)
    boost = ranking
    for power in range(3):
        boost = boost * boost // amount
    boost = boost * lift // amount
    tickets = jax.random.randint(jax.random.fold_in(stream_key, 2), (rows, amount), 0, 4096) + boost
    fixed_rows = jax.random.permutation(jax.random.fold_in(stream_key, 3), rows)[jnp.arange(amount) % rows]
    tickets = jnp.where(jnp.arange(rows)[:, None] == fixed_rows[None, :], 1 << 14, tickets)
    merit = tickets * amount + jnp.arange(amount)
    return lax.top_k(merit.astype(jnp.int32), top)[1].astype(jnp.int32)


def scatter_about(key, extent, deviation, limit, split=(), held_as=jnp.bfloat16):
    drawn = deviation * jax.random.normal(key, extent, jnp.float32)
    if split:
        drawn = drawn * levels(key, extent, split, -0.22, 0.18)
    return jnp.clip(drawn, -limit, limit).astype(held_as)


def setup_inputs(seed: int = 0) -> dict:
    seeds = jax.random.split(jax.random.key(seed), 9)
    wavefunction = scatter_about(seeds[0], (2, BOND, PHYS, BOND), 1.0, 6.0, ((1, 4),), jnp.float32)
    left_blocks = scatter_about(seeds[1], (K, 2, BOND, MB), (2 * MB * K) ** -0.5, 0.125, ((0, 8), (2, 4)), jnp.float32)
    right_operators = scatter_about(seeds[2], (K, 2, BOND, BOND), (2 * BOND) ** -0.5, 0.1875, ((0, 8),), jnp.float32)
    site_operators = scatter_about(seeds[3], (K, 2, PHYS, PHYS), (2 * PHYS) ** -0.5, 1.0, ((0, 8),), jnp.float32)
    term_charge = plant(jax.random.randint(seeds[4], (K,), 0, 2), jax.random.fold_in(seeds[4], 1), 0, 1).astype(jnp.int32)
    source_terms = distinct(seeds[5], K, K, TOP, 0)
    coupling = scatter_about(seeds[6], (2, K, TOP), (12 * PHYS * BOND) ** -0.5, 0.01953125, (), jnp.float32)
    owner = jax.random.permutation(seeds[7], K).astype(jnp.int32)
    return {"wavefunction": wavefunction, "left_blocks": left_blocks, "right_operators": right_operators, "site_operators": site_operators, "term_charge": term_charge, "source_terms": source_terms, "coupling": coupling, "owner": owner}


def matmul(former, latter):
    return jnp.dot(former, latter, precision=lax.Precision.HIGHEST, preferred_element_type=jnp.float32)


def contract(pattern, former, latter):
    return jnp.einsum(pattern, former, latter, precision=lax.Precision.HIGHEST, preferred_element_type=jnp.float32)


def reference(wavefunction, left_blocks, right_operators, site_operators, term_charge, source_terms, coupling, owner):
    bands = BOND // MB
    flat_re = wavefunction[0].reshape(BOND * PHYS, BOND)
    flat_im = wavefunction[1].reshape(BOND * PHYS, BOND)
    band_re = wavefunction[0].reshape(bands, MB, PHYS * BOND)
    band_im = wavefunction[1].reshape(bands, MB, PHYS * BOND)

    def one_term(running, inputs):
        right_pair, site_pair, left_pair, charge = inputs
        mixed_re = (matmul(flat_re, right_pair[0]) - matmul(flat_im, right_pair[1])).reshape(BOND, PHYS, BOND)
        mixed_im = (matmul(flat_re, right_pair[1]) + matmul(flat_im, right_pair[0])).reshape(BOND, PHYS, BOND)
        acted_re = contract("st,atb->asb", site_pair[0], mixed_re) - contract("st,atb->asb", site_pair[1], mixed_im)
        acted_im = contract("st,atb->asb", site_pair[0], mixed_im) + contract("st,atb->asb", site_pair[1], mixed_re)
        acted_re = acted_re.reshape(bands, MB, PHYS * BOND)
        acted_im = acted_im.reshape(bands, MB, PHYS * BOND)
        left_re = left_pair[0].reshape(bands, MB, MB)
        left_im = left_pair[1].reshape(bands, MB, MB)
        part_re = contract("sae,sex->sax", left_re, acted_re) - contract("sae,sex->sax", left_im, acted_im)
        part_im = contract("sae,sex->sax", left_re, acted_im) + contract("sae,sex->sax", left_im, acted_re)
        contrib = jnp.stack((part_re, part_im))
        zero_band = jnp.zeros((2, 1, MB, PHYS * BOND), jnp.float32)
        lifted = jnp.concatenate((zero_band, contrib[:, :-1]), axis=1)
        running = running + jnp.where(charge == 1, lifted, contrib)
        renorm_re = contract("sax,sex->sae", acted_re, band_re) + contract("sax,sex->sae", acted_im, band_im)
        renorm_im = contract("sax,sex->sae", acted_im, band_re) - contract("sax,sex->sae", acted_re, band_im)
        renorm = jnp.stack((renorm_re, renorm_im)).reshape(2, BOND, MB)
        return running, renorm

    start = jnp.zeros((2, bands, MB, PHYS * BOND), jnp.float32)
    total, renorms = lax.scan(one_term, start, (right_operators, site_operators, left_blocks, term_charge))
    sigma = total.reshape(2, BOND, PHYS, BOND)
    term_ids = jnp.arange(K, dtype=jnp.int32)
    selector = (source_terms[:, :, None] == term_ids[None, None, :]).astype(jnp.float32)
    weight_re = contract("jt,jtk->jk", coupling[0], selector)
    weight_im = contract("jt,jtk->jk", coupling[1], selector)
    new_re = contract("jk,kae->jae", weight_re, renorms[:, 0]) - contract("jk,kae->jae", weight_im, renorms[:, 1])
    new_im = contract("jk,kae->jae", weight_re, renorms[:, 1]) + contract("jk,kae->jae", weight_im, renorms[:, 0])
    new_terms = jnp.stack((new_re, new_im), axis=1)
    placed = (owner[None, :] == term_ids[:, None]).astype(jnp.float32)
    new_right = contract("gj,jcae->gcae", placed, new_terms)
    return sigma, new_right
```

```python
import jax
import jax.numpy as jnp
from jax import lax
from jax.sharding import PartitionSpec as P

HIGH = lax.Precision.HIGH


def ein(pattern, former, latter, precision=HIGH):
    return jnp.einsum(pattern, former, latter, precision=precision, preferred_element_type=jnp.float32)


def body(wave, left, right, site, charge, source, coupling, owner):
    _, rows, phys, bond = wave.shape
    terms = lax.axis_size("terms")
    bands = lax.axis_size("sect")
    me = lax.axis_index("terms")
    band = lax.axis_index("sect")
    cols = bond // terms
    part = bond // bands
    mine = lax.dynamic_slice_in_dim(right[0], band * part, part, axis=1)
    mine = lax.all_to_all(mine.reshape(2, part, terms, cols), "terms", 2, 2, tiled=True)
    ops = lax.all_gather(mine, "sect", axis=1, tiled=True)
    ops = ops.reshape(2, bond, terms * cols)
    lefts = lax.all_gather(left, "terms", axis=0, tiled=True)
    sites = lax.all_gather(site, "terms", axis=0, tiled=True)
    re, im = wave[0].reshape(rows * phys, bond), wave[1].reshape(rows * phys, bond)
    x_re = (ein("rb,bc->rc", re, ops[0]) - ein("rb,bc->rc", im, ops[1])).reshape(rows, phys, terms, cols)
    x_im = (ein("rb,bc->rc", re, ops[1]) + ein("rb,bc->rc", im, ops[0])).reshape(rows, phys, terms, cols)
    x = jnp.stack((x_re, x_im))
    s_re, s_im = sites[:, 0], sites[:, 1]
    s = jnp.stack((jnp.stack((s_re, -s_im), 1), jnp.stack((s_im, s_re), 1)), 1)
    y = ein("kuvpq,vaqkc->kuapc", s, x)
    y = y.reshape(terms, 2 * rows, phys * cols)
    l_re, l_im = lefts[:, 0], lefts[:, 1]
    l = jnp.concatenate((jnp.concatenate((l_re, -l_im), 2), jnp.concatenate((l_im, l_re), 2)), 1)
    raised = (charge == 1).astype(jnp.float32)
    c = ein("kae,kex->kax", l, y)
    up = jnp.einsum("kax,k->ax", c, raised, precision=lax.Precision.HIGHEST)
    stay = jnp.sum(c * (1 - raised)[:, None, None], axis=0)
    moved = lax.ppermute(up, "sect", [(i, i + 1) for i in range(bands - 1)])
    sigma = (stay + moved).reshape(2, rows, phys, cols)
    local = lax.dynamic_slice_in_dim(wave, me * cols, cols, axis=3)
    local = local.reshape(2 * rows, phys * cols)
    g = ein("kax,ex->kae", y, local).reshape(terms, 2, rows, 2, rows)
    q_re = g[:, 0, :, 0] + g[:, 1, :, 1]
    q_im = g[:, 1, :, 0] - g[:, 0, :, 1]
    term_ids = jnp.arange(terms, dtype=jnp.int32)
    hit = (source[:, :, None] == term_ids).astype(jnp.float32)
    place = (owner[None, :] == term_ids[:, None]).astype(jnp.float32)
    top = lax.Precision.HIGHEST
    w_re = ein("gj,jk->gk", place, ein("jt,jtk->jk", coupling[0], hit, top), top)
    w_im = ein("gj,jk->gk", place, ein("jt,jtk->jk", coupling[1], hit, top), top)
    n_re = ein("gk,kae->gae", w_re, q_re) - ein("gk,kae->gae", w_im, q_im)
    n_im = ein("gk,kae->gae", w_re, q_im) + ein("gk,kae->gae", w_im, q_re)
    new = lax.psum_scatter(jnp.stack((n_re, n_im), 1), "terms", scatter_dimension=0, tiled=True)
    return sigma, new


def solution(mesh):
    placed = (
        P(None, "sect", None, None),
        P("terms", None, "sect", None),
        P("terms", None, None, None),
        P("terms", None, None, None),
        P(),
        P(),
        P(),
        P(),
    )
    return jax.shard_map(
        body,
        mesh=mesh,
        in_specs=placed,
        out_specs=(P(None, "sect", None, "terms"), P("terms", None, "sect", None)),
        check_vma=False,
    )
```

```python
import functools

import jax
import jax.numpy as jnp
from jax import lax
from jax.experimental import pallas as pl
from jax.experimental.pallas import tpu as pltpu
from jax.sharding import PartitionSpec as P

LANES = 128


def split(value):
    high = value.astype(jnp.bfloat16)
    return high, (value - high.astype(jnp.float32)).astype(jnp.bfloat16)


def triple(former, latter, dims=(((1,), (0,)), ((), ()))):
    dot = functools.partial(lax.dot_general, dimension_numbers=dims, preferred_element_type=jnp.float32)
    return dot(former[0], latter[0]) + dot(former[0], latter[1]) + dot(former[1], latter[0])


def act_kernel(wave_ref, ops_ref, coef_ref, y_ref, high, low, mixed):
    groups, _, phys, rows, _ = y_ref.shape

    @pl.when(pl.program_id(0) == 0)
    def _():
        both = (ops_ref[0], ops_ref[1], ops_ref[0] + ops_ref[1])
        for j, value in enumerate(both):
            high[j], low[j] = split(value)

    re, im = wave_ref[0], wave_ref[1]
    t = [triple(split(v), (high[j], low[j])) for j, v in enumerate((re, im, re + im))]
    for j, value in enumerate((t[0] - t[1], t[2] - t[0] - t[1], t[2] - 2.0 * t[1])):
        for g in range(groups):
            mixed[j, g] = value[:, g * LANES : (g + 1) * LANES]

    def block(step, carry):
        g, r = step // (rows // 8), step % (rows // 8)
        base = pl.multiple_of(r * 8 * phys, 8 * phys)
        x = [[mixed[j, g, pl.ds(base + q, 8, stride=phys), :] for q in range(phys)] for j in range(3)]
        out = pl.ds(pl.multiple_of(r * 8, 8), 8)
        for p in range(phys):
            s = []
            for j in range(3):
                total = coef_ref[j, g, p, 0:1, :] * x[j][0]
                for q in range(1, phys):
                    total = total + coef_ref[j, g, p, q : q + 1, :] * x[j][q]
                s.append(total)
            y_ref[g, 0, p, out, :] = s[0] - s[1]
            y_ref[g, 1, p, out, :] = s[2] - s[0] - s[1]
        return carry

    lax.fori_loop(0, groups * (rows // 8), block, 0)


def act(wave, ops, coef, phys):
    _, flat, bond = wave.shape
    rows = flat // phys
    width = ops.shape[2]
    groups = width // LANES
    step = 32
    return pl.pallas_call(
        act_kernel,
        grid=(rows // step,),
        in_specs=[
            pl.BlockSpec((2, step * phys, bond), lambda i: (0, i, 0)),
            pl.BlockSpec((2, bond, width), lambda i: (0, 0, 0)),
            pl.BlockSpec(coef.shape, lambda i: (0, 0, 0, 0, 0)),
        ],
        out_specs=pl.BlockSpec((groups, 2, phys, step, LANES), lambda i: (0, 0, 0, i, 0)),
        out_shape=jax.ShapeDtypeStruct((groups, 2, phys, rows, LANES), jnp.float32),
        scratch_shapes=[
            pltpu.VMEM((3, bond, width), jnp.bfloat16),
            pltpu.VMEM((3, bond, width), jnp.bfloat16),
            pltpu.VMEM((3, groups, step * phys, LANES), jnp.float32),
        ],
        compiler_params=pltpu.CompilerParams(vmem_limit_bytes=60 * 1024 * 1024),
    )(wave, ops, coef)


def close_kernel(charge_ref, y_ref, left_ref, local_ref, stay_ref, up_ref, gram_ref, high, low):
    per = left_ref.shape[0]
    phys = y_ref.shape[2]
    cols = LANES // per
    group = pl.program_id(0)

    @pl.when(group == 0)
    def _():
        high[...], low[...] = split(local_ref[...])
        stay_ref[...] = jnp.zeros_like(stay_ref)
        up_ref[...] = jnp.zeros_like(up_ref)

    for j in range(per):
        y = jnp.concatenate(
            [
                jnp.concatenate([y_ref[0, h, p, :, j * cols : (j + 1) * cols] for p in range(phys)], axis=1)
                for h in range(2)
            ],
            axis=0,
        )
        y = split(y)
        gram_ref[j] = triple(y, (high[...], low[...]), (((1,), (1,)), ((), ())))
        c = triple(split(left_ref[j]), y)
        raised = (charge_ref[group * per + j] == 1).astype(jnp.float32)
        up_ref[...] += c * raised
        stay_ref[...] += c * (1.0 - raised)


def close(charge, y, left, local):
    groups, _, phys, rows, _ = y.shape
    terms, tall, _ = left.shape
    per = terms // groups
    wide = local.shape[1]
    fixed = pl.BlockSpec((tall, wide), lambda i: (0, 0))
    return pl.pallas_call(
        close_kernel,
        grid=(groups,),
        in_specs=[
            pl.BlockSpec(memory_space=pltpu.SMEM),
            pl.BlockSpec((1, 2, phys, rows, LANES), lambda i: (i, 0, 0, 0, 0)),
            pl.BlockSpec((per, tall, tall), lambda i: (i, 0, 0)),
            fixed,
        ],
        out_specs=[fixed, fixed, pl.BlockSpec((per, tall, tall), lambda i: (i, 0, 0))],
        out_shape=[
            jax.ShapeDtypeStruct((tall, wide), jnp.float32),
            jax.ShapeDtypeStruct((tall, wide), jnp.float32),
            jax.ShapeDtypeStruct((terms, tall, tall), jnp.float32),
        ],
        scratch_shapes=[pltpu.VMEM((tall, wide), jnp.bfloat16)] * 2,
        compiler_params=pltpu.CompilerParams(vmem_limit_bytes=60 * 1024 * 1024),
    )(charge, y, left, local)

HIGH = lax.Precision.HIGH


def ein(pattern, former, latter, precision=HIGH):
    return jnp.einsum(pattern, former, latter, precision=precision, preferred_element_type=jnp.float32)


def body(wave, left, right, site, charge, source, coupling, owner):
    _, rows, phys, bond = wave.shape
    terms = lax.axis_size("terms")
    bands = lax.axis_size("sect")
    me = lax.axis_index("terms")
    band = lax.axis_index("sect")
    cols = bond // terms
    part = bond // bands
    mine = lax.dynamic_slice_in_dim(right[0], band * part, part, axis=1)
    mine = lax.all_to_all(mine.reshape(2, part, terms, cols), "terms", 2, 2, tiled=True)
    ops = lax.all_gather(mine, "sect", axis=1, tiled=True)
    ops = ops.reshape(2, bond, terms * cols)
    lefts = lax.all_gather(left, "terms", axis=0, tiled=True)
    sites = lax.all_gather(site, "terms", axis=0, tiled=True)
    weights = jnp.stack((sites[:, 0], sites[:, 1], sites[:, 0] + sites[:, 1]))
    coef = jnp.repeat(weights.transpose(0, 2, 3, 1), cols, axis=3)
    coef = coef.reshape(3, phys, phys, -1, LANES).transpose(0, 3, 1, 2, 4)
    y = act(wave.reshape(2, rows * phys, bond), ops, coef, phys)
    l_re, l_im = lefts[:, 0], lefts[:, 1]
    l = jnp.concatenate((jnp.concatenate((l_re, -l_im), 2), jnp.concatenate((l_im, l_re), 2)), 1)
    local = lax.dynamic_slice_in_dim(wave, me * cols, cols, axis=3).reshape(2 * rows, phys * cols)
    stay, up, g = close(charge, y, l, local)
    moved = lax.ppermute(up, "sect", [(i, i + 1) for i in range(bands - 1)])
    sigma = (stay + moved).reshape(2, rows, phys, cols)
    g = g.reshape(terms, 2, rows, 2, rows)
    q_re = g[:, 0, :, 0] + g[:, 1, :, 1]
    q_im = g[:, 1, :, 0] - g[:, 0, :, 1]
    term_ids = jnp.arange(terms, dtype=jnp.int32)
    hit = (source[:, :, None] == term_ids).astype(jnp.float32)
    place = (owner[None, :] == term_ids[:, None]).astype(jnp.float32)
    top = lax.Precision.HIGHEST
    w_re = ein("gj,jk->gk", place, ein("jt,jtk->jk", coupling[0], hit, top), top)
    w_im = ein("gj,jk->gk", place, ein("jt,jtk->jk", coupling[1], hit, top), top)
    n_re = ein("gk,kae->gae", w_re, q_re) - ein("gk,kae->gae", w_im, q_im)
    n_im = ein("gk,kae->gae", w_re, q_im) + ein("gk,kae->gae", w_im, q_re)
    new = lax.psum_scatter(jnp.stack((n_re, n_im), 1), "terms", scatter_dimension=0, tiled=True)
    return sigma, new


def solution(mesh):
    placed = (
        P(None, "sect", None, None),
        P("terms", None, "sect", None),
        P("terms", None, None, None),
        P("terms", None, None, None),
        P(),
        P(),
        P(),
        P(),
    )
    return jax.shard_map(
        body,
        mesh=mesh,
        in_specs=placed,
        out_specs=(P(None, "sect", None, "terms"), P("terms", None, "sect", None)),
        check_vma=False,
    )
```

```python
import functools

import jax
import jax.numpy as jnp
from jax import lax
from jax.experimental import pallas as pl
from jax.experimental.pallas import tpu as pltpu
from jax.sharding import PartitionSpec as P

LANES = 128


def split(value):
    high = value.astype(jnp.bfloat16)
    return high, (value - high.astype(jnp.float32)).astype(jnp.bfloat16)


def triple(former, latter, dims=(((1,), (0,)), ((), ()))):
    dot = functools.partial(lax.dot_general, dimension_numbers=dims, preferred_element_type=jnp.float32)
    return dot(former[0], latter[0]) + dot(former[0], latter[1]) + dot(former[1], latter[0])


def act_kernel(wave_ref, ops_ref, coef_ref, y_ref, high, low, mixed):
    groups, _, phys, rows, _ = y_ref.shape

    @pl.when(pl.program_id(0) == 0)
    def _():
        per = ops_ref.shape[0] // groups
        cols = LANES // per
        deep = ops_ref.shape[2]
        for g in range(groups):
            lanes = slice(g * LANES, (g + 1) * LANES)
            for i in range(per):
                part = [
                    jnp.concatenate(
                        [ops_ref[g * per + j, h, :, i * cols : (i + 1) * cols] for j in range(per)], axis=1
                    )
                    for h in range(2)
                ]
                for j, value in enumerate((part[0], part[1], part[0] + part[1])):
                    spot = (j, slice(i * deep, (i + 1) * deep), lanes)
                    high[spot], low[spot] = split(value)

    re, im = wave_ref[0], wave_ref[1]
    t = [triple(split(v), (high[j], low[j])) for j, v in enumerate((re, im, re + im))]
    for j, value in enumerate((t[0] - t[1], t[2] - t[0] - t[1], t[2] - 2.0 * t[1])):
        for g in range(groups):
            mixed[j, g] = value[:, g * LANES : (g + 1) * LANES]

    def block(step, carry):
        g, r = step // (rows // 8), step % (rows // 8)
        base = pl.multiple_of(r * 8 * phys, 8 * phys)
        x = [[mixed[j, g, pl.ds(base + q, 8, stride=phys), :] for q in range(phys)] for j in range(3)]
        out = pl.ds(pl.multiple_of(r * 8, 8), 8)
        for p in range(phys):
            s = []
            for j in range(3):
                total = coef_ref[j, g, p, 0:1, :] * x[j][0]
                for q in range(1, phys):
                    total = total + coef_ref[j, g, p, q : q + 1, :] * x[j][q]
                s.append(total)
            y_ref[g, 0, p, out, :] = s[0] - s[1]
            y_ref[g, 1, p, out, :] = s[2] - s[0] - s[1]
        return carry

    lax.fori_loop(0, groups * (rows // 8), block, 0)


def act(wave, ops, coef, phys):
    _, flat, bond = wave.shape
    rows = flat // phys
    groups = coef.shape[1]
    width = groups * LANES
    step = 32
    return pl.pallas_call(
        act_kernel,
        grid=(rows // step,),
        in_specs=[
            pl.BlockSpec((2, step * phys, bond), lambda i: (0, i, 0)),
            pl.BlockSpec(ops.shape, lambda i: (0, 0, 0, 0)),
            pl.BlockSpec(coef.shape, lambda i: (0, 0, 0, 0, 0)),
        ],
        out_specs=pl.BlockSpec((groups, 2, phys, step, LANES), lambda i: (0, 0, 0, i, 0)),
        out_shape=jax.ShapeDtypeStruct((groups, 2, phys, rows, LANES), jnp.float32),
        scratch_shapes=[
            pltpu.VMEM((3, bond, width), jnp.bfloat16),
            pltpu.VMEM((3, bond, width), jnp.bfloat16),
            pltpu.VMEM((3, groups, step * phys, LANES), jnp.float32),
        ],
        compiler_params=pltpu.CompilerParams(vmem_limit_bytes=60 * 1024 * 1024),
    )(wave, ops, coef)


def close_kernel(charge_ref, weight_ref, y_ref, left_ref, local_ref, stay_ref, up_ref, new_ref, high, low):
    per = left_ref.shape[0]
    terms = new_ref.shape[0]
    phys, rows = y_ref.shape[2], y_ref.shape[3]
    cols = LANES // per
    group = pl.program_id(0)

    @pl.when(group == 0)
    def _():
        high[...], low[...] = split(local_ref[...])
        stay_ref[...] = jnp.zeros_like(stay_ref)
        up_ref[...] = jnp.zeros_like(up_ref)
        new_ref[...] = jnp.zeros_like(new_ref)

    for j in range(per):
        term = group * per + j
        y = jnp.concatenate(
            [
                jnp.concatenate([y_ref[0, h, p, :, j * cols : (j + 1) * cols] for p in range(phys)], axis=1)
                for h in range(2)
            ],
            axis=0,
        )
        y = split(y)
        re, im = left_ref[j, :rows], left_ref[j, rows : 2 * rows]
        left = jnp.concatenate(
            [jnp.concatenate([re, -im], axis=1), jnp.concatenate([im, re], axis=1)], axis=0
        )
        c = triple(split(left), y)
        raised = (charge_ref[term] == 1).astype(jnp.float32)
        up_ref[...] += c * raised
        stay_ref[...] += c * (1.0 - raised)
        gram = triple(y, (high[...], low[...]), (((1,), (1,)), ((), ())))
        q_re = gram[:rows, :rows] + gram[rows:, rows:]
        q_im = gram[rows:, :rows] - gram[:rows, rows:]

        def add(g, carry):
            w_re, w_im = weight_ref[0, g, term], weight_ref[1, g, term]
            new_ref[g, :rows, :] += w_re * q_re - w_im * q_im
            new_ref[g, rows:, :] += w_re * q_im + w_im * q_re
            return carry

        lax.fori_loop(0, terms, add, 0)


def close(charge, weight, y, left, local):
    groups, _, phys, rows, _ = y.shape
    terms, lines, _ = left.shape
    per = terms // groups
    tall, wide = local.shape
    fixed = pl.BlockSpec((tall, wide), lambda i: (0, 0))
    return pl.pallas_call(
        close_kernel,
        grid=(groups,),
        in_specs=[
            pl.BlockSpec(memory_space=pltpu.SMEM),
            pl.BlockSpec(memory_space=pltpu.SMEM),
            pl.BlockSpec((1, 2, phys, rows, LANES), lambda i: (i, 0, 0, 0, 0)),
            pl.BlockSpec((per, lines, rows), lambda i: (i, 0, 0)),
            fixed,
        ],
        out_specs=[fixed, fixed, pl.BlockSpec((terms, tall, rows), lambda i: (0, 0, 0))],
        out_shape=[
            jax.ShapeDtypeStruct((tall, wide), jnp.float32),
            jax.ShapeDtypeStruct((tall, wide), jnp.float32),
            jax.ShapeDtypeStruct((terms, tall, rows), jnp.float32),
        ],
        scratch_shapes=[pltpu.VMEM((tall, wide), jnp.bfloat16)] * 2,
        compiler_params=pltpu.CompilerParams(vmem_limit_bytes=60 * 1024 * 1024),
    )(charge, weight, y, left, local)


def remote(source, target, sends, lands, place):
    return pltpu.make_async_remote_copy(
        src_ref=source,
        dst_ref=target,
        send_sem=sends,
        recv_sem=lands,
        device_id=place,
        device_id_type=pl.DeviceIdType.MESH,
    )


def greet(places):
    barrier = pltpu.get_barrier_semaphore()
    for place in places:
        pl.semaphore_signal(barrier, inc=1, device_id=place, device_id_type=pl.DeviceIdType.MESH)
    pl.semaphore_wait(barrier, len(places))


def gather_kernel(pack_ref, small_ref, ops_ref, smalls_ref, send_a, land_a, send_x, land_x, send_c, land_c, send_f, land_f, send_s, land_s, send_t, land_t, own):
    terms, bands = pack_ref.shape[:2]
    half = terms // 2
    me = lax.axis_index("terms")
    band = lax.axis_index("sect")
    twin = me + 1 - 2 * lax.rem(me, 2)
    near = band + 1 - 2 * lax.rem(band, 2)
    far = lax.rem(band + 2, 4)
    greet([(lax.rem(me + i, terms), band) for i in range(1, terms)] + [(me, near), (me, far)])
    keep = pltpu.make_async_copy(pack_ref.at[me], ops_ref.at[me], own.at[0])
    keep.start()
    keep_small = pltpu.make_async_copy(small_ref, smalls_ref.at[me], own.at[1])
    keep_small.start()
    first = []
    for i in range(1, terms):
        peer = lax.rem(me + i, terms)
        copy = remote(pack_ref.at[peer, band], ops_ref.at[me, band], send_a.at[i - 1], land_a.at[i - 1], (peer, band))
        copy.start()
        first.append(copy)
    tiny = []
    for i in range(half):
        place = (twin if i == 0 else lax.rem(me + 2 * i, terms), band)
        copy = remote(small_ref, smalls_ref.at[me], send_s.at[i], land_s.at[i], place)
        copy.start()
        tiny.append(copy)
    across, beside = [], []
    for i in range(1, terms):
        first[i - 1].wait_recv()
        block = ops_ref.at[lax.rem(me + terms - i, terms), band]
        copy = remote(block, block, send_x.at[i - 1], land_x.at[i - 1], (me, far))
        copy.start()
        across.append(copy)
        copy = remote(block, block, send_c.at[i - 1], land_c.at[i - 1], (me, near))
        copy.start()
        beside.append(copy)
    relay = []
    for i in range(1, half):
        tiny[i].wait_recv()
        block = smalls_ref.at[lax.rem(me + terms - 2 * i, terms)]
        copy = remote(block, block, send_t.at[i - 1], land_t.at[i - 1], (twin, band))
        copy.start()
        relay.append(copy)
    last = []
    for i in range(1, terms):
        across[i - 1].wait_recv()
        block = ops_ref.at[lax.rem(me + terms - i, terms), far]
        copy = remote(block, block, send_f.at[i - 1], land_f.at[i - 1], (me, near))
        copy.start()
        last.append(copy)
    for copy in beside + last + relay + tiny[:1]:
        copy.wait_recv()
    for copy in first + tiny + across + beside + relay + last:
        copy.wait_send()
    keep.wait()
    keep_small.wait()


def gather(pack, small):
    terms = pack.shape[0]
    vmem = pl.BlockSpec(memory_space=pltpu.VMEM)
    pair = [pltpu.SemaphoreType.DMA((terms - 1,))] * 2
    return pl.pallas_call(
        gather_kernel,
        in_specs=[vmem, vmem],
        out_specs=[vmem, vmem],
        out_shape=[
            jax.ShapeDtypeStruct(pack.shape, jnp.float32),
            jax.ShapeDtypeStruct((terms,) + small.shape, jnp.float32),
        ],
        scratch_shapes=pair * 6 + [pltpu.SemaphoreType.DMA((2,))],
        compiler_params=pltpu.CompilerParams(
            collective_id=0, has_side_effects=True, vmem_limit_bytes=40 * 1024 * 1024
        ),
    )(pack, small)


def finish_kernel(stay_ref, up_ref, part_ref, sigma_ref, new_ref, moved, got, send_a, land_a, edge):
    terms = part_ref.shape[0]
    me = lax.axis_index("terms")
    band = lax.axis_index("sect")
    bands = lax.axis_size("sect")
    upper = lax.rem(band + 1, bands)
    lower = lax.rem(band + bands - 1, bands)
    greet([(lax.rem(me + i, terms), band) for i in range(1, terms)] + [(me, upper), (me, lower)])
    shift = remote(up_ref, moved, edge.at[0], edge.at[1], (me, upper))
    shift.start()
    copies = []
    for i in range(1, terms):
        peer = lax.rem(me + i, terms)
        copy = remote(part_ref.at[peer], got.at[i - 1], send_a.at[i - 1], land_a.at[i - 1], (peer, band))
        copy.start()
        copies.append(copy)
    shift.wait()
    sigma_ref[...] = stay_ref[...] + jnp.where(band > 0, moved[...], 0.0)
    total = part_ref[me]
    for i, copy in enumerate(copies):
        copy.wait()
        total = total + got[i]
    new_ref[...] = total


def finish(stay, up, part):
    terms = part.shape[0]
    vmem = pl.BlockSpec(memory_space=pltpu.VMEM)
    return pl.pallas_call(
        finish_kernel,
        in_specs=[vmem] * 3,
        out_specs=[vmem] * 2,
        out_shape=[
            jax.ShapeDtypeStruct(stay.shape, jnp.float32),
            jax.ShapeDtypeStruct(part.shape[1:], jnp.float32),
        ],
        scratch_shapes=[
            pltpu.VMEM(stay.shape, jnp.float32),
            pltpu.VMEM((terms - 1,) + part.shape[1:], jnp.float32),
            pltpu.SemaphoreType.DMA((terms - 1,)),
            pltpu.SemaphoreType.DMA((terms - 1,)),
            pltpu.SemaphoreType.DMA((2,)),
        ],
        compiler_params=pltpu.CompilerParams(
            collective_id=1, has_side_effects=True, vmem_limit_bytes=40 * 1024 * 1024
        ),
    )(stay, up, part)


def body(wave, left, right, site, charge, source, coupling, owner):
    _, rows, phys, bond = wave.shape
    terms = lax.axis_size("terms")
    bands = lax.axis_size("sect")
    me = lax.axis_index("terms")
    cols = bond // terms
    per = LANES // cols
    pack = right[0].reshape(2, per, bond // per, terms, cols).transpose(3, 0, 2, 1, 4)
    pack = pack.reshape(terms, bands, -1, LANES)
    lines = site.size // LANES
    room = -lines % 8
    small = jnp.concatenate(
        (left[0].reshape(2 * rows, rows), site.reshape(lines, LANES), jnp.zeros((room, LANES), jnp.float32))
    )
    ops, smalls = gather(pack, small)
    sites = smalls[:, 2 * rows : 2 * rows + lines].reshape(terms // per, per, 2, phys, phys)
    weights = jnp.stack((sites[:, :, 0], sites[:, :, 1], sites[:, :, 0] + sites[:, :, 1]))
    slot = jnp.arange(LANES, dtype=jnp.int32) // cols
    coef = sum(jnp.where(slot == j, weights[:, :, j, :, :, None], 0.0) for j in range(per))
    y = act(wave.reshape(2, rows * phys, bond), ops.reshape(terms, 2, bond // per, LANES), coef, phys)
    local = lax.dynamic_slice_in_dim(wave, me * cols, cols, axis=3).reshape(2 * rows, phys * cols)
    term_ids = jnp.arange(terms, dtype=jnp.int32)
    hit = (source[:, :, None] == term_ids).astype(jnp.float32)
    place = (owner[None, :] == term_ids[:, None]).astype(jnp.float32)
    weight = jnp.sum(coupling[:, :, :, None] * hit, axis=2)
    weight = jnp.sum(place[None, :, :, None] * weight[:, None], axis=2)
    stay, up, part = close(charge, weight, y, smalls, local)
    sigma, new = finish(stay, up, part)
    return sigma.reshape(2, rows, phys, cols), new.reshape(1, 2, rows, rows)


def solution(mesh):
    placed = (
        P(None, "sect", None, None),
        P("terms", None, "sect", None),
        P("terms", None, None, None),
        P("terms", None, None, None),
        P(),
        P(),
        P(),
        P(),
    )
    return jax.shard_map(
        body,
        mesh=mesh,
        in_specs=placed,
        out_specs=(P(None, "sect", None, "terms"), P("terms", None, "sect", None)),
        check_vma=False,
    )
```

```python
import functools

import jax
import jax.numpy as jnp
from jax import lax
from jax.experimental import pallas as pl
from jax.experimental.pallas import tpu as pltpu
from jax.sharding import PartitionSpec as P

LANES = 128


def split(value):
    high = value.astype(jnp.bfloat16)
    return high, (value - high.astype(jnp.float32)).astype(jnp.bfloat16)


def triple(former, latter, dims=(((1,), (0,)), ((), ()))):
    dot = functools.partial(lax.dot_general, dimension_numbers=dims, preferred_element_type=jnp.float32)
    return dot(former[0], latter[0]) + dot(former[0], latter[1]) + dot(former[1], latter[0])


def act_kernel(wave_ref, ops_ref, coef_ref, y_ref, high, low, mixed):
    groups, _, phys, rows, _ = y_ref.shape

    @pl.when(pl.program_id(0) == 0)
    def _():
        per = ops_ref.shape[0] // groups
        cols = LANES // per
        deep = ops_ref.shape[2]
        for g in range(groups):
            lanes = slice(g * LANES, (g + 1) * LANES)
            for i in range(per):
                part = [
                    jnp.concatenate(
                        [ops_ref[g * per + j, h, :, i * cols : (i + 1) * cols] for j in range(per)], axis=1
                    )
                    for h in range(2)
                ]
                for j, value in enumerate((part[0], part[1], part[0] + part[1])):
                    spot = (j, slice(i * deep, (i + 1) * deep), lanes)
                    high[spot], low[spot] = split(value)

    re, im = wave_ref[0], wave_ref[1]
    t = [triple(split(v), (high[j], low[j])) for j, v in enumerate((re, im, re + im))]
    for j, value in enumerate((t[0] - t[1], t[2] - t[0] - t[1], t[2] - 2.0 * t[1])):
        for g in range(groups):
            mixed[j, g] = value[:, g * LANES : (g + 1) * LANES]

    def block(step, carry):
        g, r = step // (rows // 8), step % (rows // 8)
        base = pl.multiple_of(r * 8 * phys, 8 * phys)
        x = [[mixed[j, g, pl.ds(base + q, 8, stride=phys), :] for q in range(phys)] for j in range(3)]
        out = pl.ds(pl.multiple_of(r * 8, 8), 8)
        for p in range(phys):
            s = []
            for j in range(3):
                total = coef_ref[j, g, p, 0:1, :] * x[j][0]
                for q in range(1, phys):
                    total = total + coef_ref[j, g, p, q : q + 1, :] * x[j][q]
                s.append(total)
            y_ref[g, 0, p, out, :] = s[0] - s[1]
            y_ref[g, 1, p, out, :] = s[2] - s[0] - s[1]
        return carry

    lax.fori_loop(0, groups * (rows // 8), block, 0)


def act(wave, ops, coef, phys):
    _, flat, bond = wave.shape
    rows = flat // phys
    groups = coef.shape[1]
    width = groups * LANES
    step = 32
    return pl.pallas_call(
        act_kernel,
        grid=(rows // step,),
        in_specs=[
            pl.BlockSpec((2, step * phys, bond), lambda i: (0, i, 0)),
            pl.BlockSpec(ops.shape, lambda i: (0, 0, 0, 0)),
            pl.BlockSpec(coef.shape, lambda i: (0, 0, 0, 0, 0)),
        ],
        out_specs=pl.BlockSpec((groups, 2, phys, step, LANES), lambda i: (0, 0, 0, i, 0)),
        out_shape=jax.ShapeDtypeStruct((groups, 2, phys, rows, LANES), jnp.float32),
        scratch_shapes=[
            pltpu.VMEM((3, bond, width), jnp.bfloat16),
            pltpu.VMEM((3, bond, width), jnp.bfloat16),
            pltpu.VMEM((3, groups, step * phys, LANES), jnp.float32),
        ],
        compiler_params=pltpu.CompilerParams(vmem_limit_bytes=58 * 1024 * 1024),
    )(wave, ops, coef)


def close_kernel(charge_ref, weight_ref, y_ref, left_ref, local_ref, stay_ref, up_ref, new_ref, high, low):
    per = left_ref.shape[0]
    terms = new_ref.shape[0]
    phys, rows = y_ref.shape[2], y_ref.shape[3]
    cols = LANES // per
    group = pl.program_id(0)

    @pl.when(group == 0)
    def _():
        high[...], low[...] = split(local_ref[...])
        stay_ref[...] = jnp.zeros_like(stay_ref)
        up_ref[...] = jnp.zeros_like(up_ref)
        new_ref[...] = jnp.zeros_like(new_ref)

    for j in range(per):
        term = group * per + j
        y = jnp.concatenate(
            [
                jnp.concatenate([y_ref[0, h, p, :, j * cols : (j + 1) * cols] for p in range(phys)], axis=1)
                for h in range(2)
            ],
            axis=0,
        )
        y = split(y)
        re, im = left_ref[j, :rows], left_ref[j, rows : 2 * rows]
        left = jnp.concatenate(
            [jnp.concatenate([re, -im], axis=1), jnp.concatenate([im, re], axis=1)], axis=0
        )
        c = triple(split(left), y)
        raised = (charge_ref[term] == 1).astype(jnp.float32)
        up_ref[...] += c * raised
        stay_ref[...] += c * (1.0 - raised)
        gram = triple(y, (high[...], low[...]), (((1,), (1,)), ((), ())))
        q_re = gram[:rows, :rows] + gram[rows:, rows:]
        q_im = gram[rows:, :rows] - gram[:rows, rows:]

        def add(g, carry):
            w_re, w_im = weight_ref[0, g, term], weight_ref[1, g, term]
            new_ref[g, :rows, :] += w_re * q_re - w_im * q_im
            new_ref[g, rows:, :] += w_re * q_im + w_im * q_re
            return carry

        lax.fori_loop(0, terms, add, 0)


def close(charge, weight, y, left, local):
    groups, _, phys, rows, _ = y.shape
    terms, lines, _ = left.shape
    per = terms // groups
    tall, wide = local.shape
    fixed = pl.BlockSpec((tall, wide), lambda i: (0, 0))
    return pl.pallas_call(
        close_kernel,
        grid=(groups,),
        in_specs=[
            pl.BlockSpec(memory_space=pltpu.SMEM),
            pl.BlockSpec(memory_space=pltpu.SMEM),
            pl.BlockSpec((1, 2, phys, rows, LANES), lambda i: (i, 0, 0, 0, 0)),
            pl.BlockSpec((per, lines, rows), lambda i: (i, 0, 0)),
            fixed,
        ],
        out_specs=[pl.BlockSpec(memory_space=pltpu.VMEM)] * 3,
        out_shape=[
            jax.ShapeDtypeStruct((tall, wide), jnp.float32),
            jax.ShapeDtypeStruct((tall, wide), jnp.float32),
            jax.ShapeDtypeStruct((terms, tall, rows), jnp.float32),
        ],
        scratch_shapes=[pltpu.VMEM((tall, wide), jnp.bfloat16)] * 2,
        compiler_params=pltpu.CompilerParams(vmem_limit_bytes=54 * 1024 * 1024),
    )(charge, weight, y, left, local)


def pack_kernel(right_ref, pack_ref):
    terms, _, deep, _ = pack_ref.shape
    cols = right_ref.shape[2] // terms
    per = LANES // cols
    for t in range(terms):
        for h in range(2):
            pieces = [right_ref[h, i * deep : (i + 1) * deep, t * cols : (t + 1) * cols] for i in range(per)]
            pack_ref[t, h] = jnp.concatenate(pieces, axis=1)


def packed(right, terms):
    _, bond, width = right.shape
    deep = bond * width // (terms * LANES)
    vmem = pl.BlockSpec(memory_space=pltpu.VMEM)
    return pl.pallas_call(
        pack_kernel,
        in_specs=[vmem],
        out_specs=vmem,
        out_shape=jax.ShapeDtypeStruct((terms, 2, deep, LANES), jnp.float32),
        compiler_params=pltpu.CompilerParams(vmem_limit_bytes=16 * 1024 * 1024),
    )(right)


def remote(source, target, sends, lands, place):
    return pltpu.make_async_remote_copy(
        src_ref=source,
        dst_ref=target,
        send_sem=sends,
        recv_sem=lands,
        device_id=place,
        device_id_type=pl.DeviceIdType.MESH,
    )


def greet(places):
    barrier = pltpu.get_barrier_semaphore()
    for place in places:
        pl.semaphore_signal(barrier, inc=1, device_id=place, device_id_type=pl.DeviceIdType.MESH)
    pl.semaphore_wait(barrier, len(places))


def gather_kernel(pack_ref, small_ref, ops_ref, smalls_ref, send_a, land_a, send_x, land_x, send_c, land_c, send_f, land_f, send_s, land_s, send_t, land_t, own):
    terms, bands = pack_ref.shape[:2]
    half = terms // 2
    me = lax.axis_index("terms")
    band = lax.axis_index("sect")
    twin = me + 1 - 2 * lax.rem(me, 2)
    near = band + 1 - 2 * lax.rem(band, 2)
    far = lax.rem(band + 2, 4)
    greet([(lax.rem(me + i, terms), band) for i in range(1, terms)] + [(me, near), (me, far)])
    keep = pltpu.make_async_copy(pack_ref.at[me], ops_ref.at[me], own.at[0])
    keep.start()
    keep_small = pltpu.make_async_copy(small_ref, smalls_ref.at[me], own.at[1])
    keep_small.start()
    first = []
    for i in range(1, terms):
        peer = lax.rem(me + i, terms)
        copy = remote(pack_ref.at[peer, band], ops_ref.at[me, band], send_a.at[i - 1], land_a.at[i - 1], (peer, band))
        copy.start()
        first.append(copy)
    tiny = []
    for i in range(half):
        place = (twin if i == 0 else lax.rem(me + 2 * i, terms), band)
        copy = remote(small_ref, smalls_ref.at[me], send_s.at[i], land_s.at[i], place)
        copy.start()
        tiny.append(copy)
    across, beside = [], []
    for i in range(1, terms):
        first[i - 1].wait_recv()
        block = ops_ref.at[lax.rem(me + terms - i, terms), band]
        copy = remote(block, block, send_x.at[i - 1], land_x.at[i - 1], (me, far))
        copy.start()
        across.append(copy)
        copy = remote(block, block, send_c.at[i - 1], land_c.at[i - 1], (me, near))
        copy.start()
        beside.append(copy)
    relay = []
    for i in range(1, half):
        tiny[i].wait_recv()
        block = smalls_ref.at[lax.rem(me + terms - 2 * i, terms)]
        copy = remote(block, block, send_t.at[i - 1], land_t.at[i - 1], (twin, band))
        copy.start()
        relay.append(copy)
    last = []
    for i in range(1, terms):
        across[i - 1].wait_recv()
        block = ops_ref.at[lax.rem(me + terms - i, terms), far]
        copy = remote(block, block, send_f.at[i - 1], land_f.at[i - 1], (me, near))
        copy.start()
        last.append(copy)
    for copy in beside + last + relay + tiny[:1]:
        copy.wait_recv()
    for copy in first + tiny + across + beside + relay + last:
        copy.wait_send()
    keep.wait()
    keep_small.wait()


def gather(pack, small):
    terms = pack.shape[0]
    vmem = pl.BlockSpec(memory_space=pltpu.VMEM)
    pair = [pltpu.SemaphoreType.DMA((terms - 1,))] * 2
    return pl.pallas_call(
        gather_kernel,
        in_specs=[vmem, vmem],
        out_specs=[vmem, vmem],
        out_shape=[
            jax.ShapeDtypeStruct(pack.shape, jnp.float32),
            jax.ShapeDtypeStruct((terms,) + small.shape, jnp.float32),
        ],
        scratch_shapes=pair * 6 + [pltpu.SemaphoreType.DMA((2,))],
        compiler_params=pltpu.CompilerParams(
            collective_id=0, has_side_effects=True, vmem_limit_bytes=24 * 1024 * 1024
        ),
    )(pack, small)


def finish_kernel(stay_ref, up_ref, part_ref, sigma_ref, new_ref, moved, got, held, mine, send_a, land_a, edge):
    terms = part_ref.shape[0]
    me = lax.axis_index("terms")
    band = lax.axis_index("sect")
    bands = lax.axis_size("sect")
    upper = lax.rem(band + 1, bands)
    lower = lax.rem(band + bands - 1, bands)
    greet([(lax.rem(me + i, terms), band) for i in range(1, terms)] + [(me, upper), (me, lower)])
    shift = remote(up_ref, moved, edge.at[0], edge.at[1], (me, upper))
    shift.start()
    copies = []
    for i in range(1, terms):
        peer = lax.rem(me + i, terms)
        copy = remote(part_ref.at[peer], got.at[i - 1], send_a.at[i - 1], land_a.at[i - 1], (peer, band))
        copy.start()
        copies.append(copy)
    keep = pltpu.make_async_copy(stay_ref, held, edge.at[2])
    keep.start()
    keep_part = pltpu.make_async_copy(part_ref.at[me], mine, edge.at[3])
    keep_part.start()
    keep.wait()
    keep_part.wait()
    shift.wait()
    sigma_ref[...] = held[...] + jnp.where(band > 0, moved[...], 0.0)
    total = mine[...]
    for i, copy in enumerate(copies):
        copy.wait()
        total = total + got[i]
    new_ref[...] = total


def finish(stay, up, part):
    terms = part.shape[0]
    vmem = pl.BlockSpec(memory_space=pltpu.VMEM)
    return pl.pallas_call(
        finish_kernel,
        in_specs=[pl.BlockSpec(memory_space=pl.ANY)] * 3,
        out_specs=[vmem] * 2,
        out_shape=[
            jax.ShapeDtypeStruct(stay.shape, jnp.float32),
            jax.ShapeDtypeStruct(part.shape[1:], jnp.float32),
        ],
        scratch_shapes=[
            pltpu.VMEM(stay.shape, jnp.float32),
            pltpu.VMEM((terms - 1,) + part.shape[1:], jnp.float32),
            pltpu.VMEM(stay.shape, jnp.float32),
            pltpu.VMEM(part.shape[1:], jnp.float32),
            pltpu.SemaphoreType.DMA((terms - 1,)),
            pltpu.SemaphoreType.DMA((terms - 1,)),
            pltpu.SemaphoreType.DMA((4,)),
        ],
        compiler_params=pltpu.CompilerParams(
            collective_id=1, has_side_effects=True, vmem_limit_bytes=24 * 1024 * 1024
        ),
    )(stay, up, part)


def body(wave, left, right, site, charge, source, coupling, owner):
    _, rows, phys, bond = wave.shape
    terms = lax.axis_size("terms")
    bands = lax.axis_size("sect")
    me = lax.axis_index("terms")
    cols = bond // terms
    per = LANES // cols
    pack = packed(right[0], terms).reshape(terms, bands, -1, LANES)
    lines = site.size // LANES
    room = -lines % 8
    small = jnp.concatenate(
        (left[0].reshape(2 * rows, rows), site.reshape(lines, LANES), jnp.zeros((room, LANES), jnp.float32))
    )
    ops, smalls = gather(pack, small)
    sites = smalls[:, 2 * rows : 2 * rows + lines].reshape(terms // per, per, 2, phys, phys)
    weights = jnp.stack((sites[:, :, 0], sites[:, :, 1], sites[:, :, 0] + sites[:, :, 1]))
    slot = jnp.arange(LANES, dtype=jnp.int32) // cols
    coef = sum(jnp.where(slot == j, weights[:, :, j, :, :, None], 0.0) for j in range(per))
    y = act(wave.reshape(2, rows * phys, bond), ops.reshape(terms, 2, bond // per, LANES), coef, phys)
    local = lax.dynamic_slice_in_dim(wave, me * cols, cols, axis=3).reshape(2 * rows, phys * cols)
    term_ids = jnp.arange(terms, dtype=jnp.int32)
    hit = (source[:, :, None] == term_ids).astype(jnp.float32)
    place = (owner[None, :] == term_ids[:, None]).astype(jnp.float32)
    weight = jnp.sum(coupling[:, :, :, None] * hit, axis=2)
    weight = jnp.sum(place[None, :, :, None] * weight[:, None], axis=2)
    stay, up, part = close(charge, weight, y, smalls, local)
    sigma, new = finish(stay, up, part)
    return sigma.reshape(2, rows, phys, cols), new.reshape(1, 2, rows, rows)


def solution(mesh):
    placed = (
        P(None, "sect", None, None),
        P("terms", None, "sect", None),
        P("terms", None, None, None),
        P("terms", None, None, None),
        P(),
        P(),
        P(),
        P(),
    )
    return jax.shard_map(
        body,
        mesh=mesh,
        in_specs=placed,
        out_specs=(P(None, "sect", None, "terms"), P("terms", None, "sect", None)),
        check_vma=False,
    )
```
